32 devices in a mesh: fn: 32 (over z, y, x, core).
Axes of the slice: x: 2, y: 2, z: 4, core: 2. Of those that a mesh axis runs over, the one named last changes fastest.
Arguments:
- support_functions: float32 [96, 64, 2048], P('fn'), may hold values from -50 to 50
- owner_counts: int32 [32], replicated, may hold values from 1 to 3, as said below
- region_shift: int32 [96], P('fn'), may hold values from 0 to 63
- kernel: float32 [64, 64], replicated, may hold values from -0.75 to 0.75
- external: float32 [131072], P('fn'), may hold values from -1 to 1
- kinetic_taps: float32 [15], replicated, may hold values from -3 to 3
- magic_taps: float32 [16], replicated, may hold values from -0.6 to 1.6
Outputs:
- filtered: float32 [64, 64, 2048], P('fn')
The draws below stay inside these ranges and needn't reach their ends.
Inputs may be any that keep to these rules, and one draw needn't show every extreme that they name: `owner_counts`: each owner's number of live slots; owners 2k and 2k+1 together hold exactly 4 live slots, so the counts sum to 64; slots at or past an owner's count hold no function.
All inputs are finite; a program needn't handle non-finite values.
Results may differ from the reference program's by a relative error of at most 0.0003.
Values sent between devices are 32-bit elements; how exact they have to be, the bound alone decides.
A program may use at most 64 MiB of HBM per device.

```python
import jax
import jax.numpy as jnp
from jax import lax

NX = 64
NY = 64
NZ = 32
KIN_HALF = 15
MAGIC = 16
CHEB = 1
FN_DEV = 2
SLOTS = 3
NF = 64
G = 131072
N_FN = 32


def draw_support_functions(key, part):
    first, second, third = jax.random.split(jax.random.fold_in(key, 17), 3)
    shape = (N_FN * SLOTS, NX, NY * NZ)
    base = jnp.clip(jax.random.normal(first, shape, jnp.float32), -5.0, 5.0)
    spread = jnp.log(10.0)
    lowest = 0.3162
    cell_scale = lowest * jnp.exp(jax.random.uniform(second, (1, NX, NY * NZ), jnp.float32, 0.0, spread))
    slot_scale = jnp.exp(jax.random.uniform(third, (N_FN * SLOTS, 1, 1), jnp.float32, 0.0, jnp.log(3.0)))
    return base * cell_scale * slot_scale


def draw_owner_counts(key, part):
    first, second = jax.random.split(jax.random.fold_in(key, 29), 2)
    pair_count = N_FN // 2
    spare = FN_DEV // 2
    moved = jax.random.randint(first, (pair_count,), -spare, spare + 1)
    forced = jax.random.randint(second, (), 0, pair_count)
    moved = jnp.where(jnp.arange(pair_count) == forced, spare, moved)
    paired = jnp.stack([FN_DEV + moved, FN_DEV - moved], axis=1)
    return paired.reshape(N_FN).astype(jnp.int32)


def draw_magic_taps(key, part):
    first, second = jax.random.split(jax.random.fold_in(key, 41), 2)
    tails = jnp.clip(jax.random.normal(first, (MAGIC,), jnp.float32) * 0.15, -0.5, 0.5)
    center = jax.random.uniform(second, (), jnp.float32, 0.8, 1.1)
    taps = jnp.where(jnp.arange(MAGIC) == MAGIC // 2, center, tails)
    return taps.astype(jnp.float32)


def plant(array, own_key, low, high):
    extent = array.shape
    place = [jax.random.randint(jax.random.fold_in(own_key, axis), (), 0, extent[axis]) for axis in range(len(extent))]
    array = array.at[tuple(place)].set(low)
    longest = extent.index(max(extent))
    place[longest] = (place[longest] + 1) % extent[longest]
    return array.at[tuple(place)].set(high)


def level_of(key, dims, cuts, smallest, high):
    def one(dim, parts):
        heights = jax.random.uniform(jax.random.fold_in(jax.random.fold_in(key, 6), dim), (parts,), jnp.float32, smallest / len(cuts), high / len(cuts))
        return jnp.repeat(jnp.exp(heights), dims[dim] // parts).reshape((-1,) + (1,) * (len(dims) - dim - 1))

    loudness = one(*cuts[0])
    for cut in cuts[1:]:
        loudness = loudness * one(*cut)
    return loudness


def gaussian(rng, extent, width, limit, held_as=jnp.bfloat16):
    entries = width * jax.random.normal(rng, extent, jnp.float32)
    return jnp.clip(entries, min=-limit, max=limit).astype(held_as)


def setup_inputs(seed: int = 0) -> dict:
    keys = jax.random.split(jax.random.key(seed), 8)
    support_functions = draw_support_functions(jax.random.fold_in(keys[7], 71), 0)
    owner_counts = draw_owner_counts(jax.random.fold_in(keys[7], 71), 0)
    region_shift = plant(jax.random.randint(keys[2], (N_FN * SLOTS,), 0, NX), jax.random.fold_in(keys[2], 1), 0, NX - 1).astype(jnp.int32)
    kernel = gaussian(keys[3], (NF, NF), NF ** -0.5, 0.75, jnp.float32)
    external = jnp.clip(jax.random.uniform(keys[4], (G,), jnp.float32, -1.0, 1.0) * level_of(keys[4], (G,), ((0, 32),), -0.4, 0.0), -1.0, 1.0)
    kinetic_taps = gaussian(keys[5], (KIN_HALF,), 0.3, 3.0, jnp.float32)
    magic_taps = draw_magic_taps(jax.random.fold_in(keys[7], 71), 0)
    return dict(support_functions=support_functions, owner_counts=owner_counts, region_shift=region_shift, kernel=kernel, external=external, kinetic_taps=kinetic_taps, magic_taps=magic_taps)


precise = lax.Precision.HIGHEST


def roll_rows(slab_rows, shift):
    length = slab_rows.shape[0]
    doubled = jnp.concatenate([slab_rows, slab_rows], axis=0)
    start_row = ((length - shift) % length).astype(jnp.int32)
    return lax.dynamic_slice_in_dim(doubled, start_row, length, 0)


def circulant(filter_taps, length):
    center = filter_taps.shape[0] // 2
    row_index = jnp.arange(length)[:, None]
    col_index = jnp.arange(length)[None, :]
    summed = jnp.zeros((length, length), filter_taps.dtype)
    for position in range(filter_taps.shape[0]):
        matches = col_index == (row_index + position - center) % length
        summed = summed + jnp.where(matches, filter_taps[position], 0.0)
    return summed


def along(matrix, values, axis_number):
    if axis_number == 1:
        return jnp.einsum("ik,fkyz->fiyz", matrix, values, precision=precise)
    if axis_number == 2:
        return jnp.einsum("ik,fxkz->fxiz", matrix, values, precision=precise)
    return jnp.einsum("ik,fxyk->fxyi", matrix, values, precision=precise)


def full_kinetic(kinetic_taps):
    return jnp.concatenate([kinetic_taps[::-1], kinetic_taps[1:]])


def potentials(mixed_rows, external):
    half = mixed_rows.shape[0] // 2
    rho_up = jnp.mean(mixed_rows[:half] ** 2, axis=0)
    rho_down = jnp.mean(mixed_rows[half:] ** 2, axis=0)
    summed = 0.5 * (rho_up + rho_down)
    spin_up = external + summed - jnp.cbrt(6.0 / jnp.pi * rho_up + 1e-6)
    spin_down = external + summed - jnp.cbrt(6.0 / jnp.pi * rho_down + 1e-6)
    return jnp.stack([spin_up, spin_down])


def spectral_bound(kinetic_taps, potential_rows):
    return 1.0 + 1.5 * jnp.sum(jnp.abs(full_kinetic(kinetic_taps))) + jnp.max(jnp.abs(potential_rows))


def chebyshev(field_rows, spin_potential, kinetic_taps, magic_taps, spectral):
    kinetic_full = full_kinetic(kinetic_taps)
    magic_norm = magic_taps / jnp.sum(jnp.abs(magic_taps))
    sizes_xyz = field_rows.shape[1:]
    kinetic_mats = [circulant(kinetic_full, sizes_xyz[index]) for index in range(3)]
    magic_mats = [circulant(magic_norm, sizes_xyz[index]) for index in range(3)]

    def apply_scaled(values):
        kinetic = along(kinetic_mats[0], values, 1) + along(kinetic_mats[1], values, 2) + along(kinetic_mats[2], values, 3)
        smooth = along(magic_mats[2], along(magic_mats[1], along(magic_mats[0], values, 1), 2), 3)
        weighted = spin_potential * smooth
        back = along(magic_mats[0].T, along(magic_mats[1].T, along(magic_mats[2].T, weighted, 3), 2), 1)
        return (-0.5 * kinetic + back) / spectral

    previous = field_rows
    current = apply_scaled(field_rows)
    for iteration in range(CHEB - 1):
        following = 2.0 * apply_scaled(current) - previous
        previous = current
        current = following
    return current


def reference(support_functions, owner_counts, region_shift, kernel, external, kinetic_taps, magic_taps):
    slot_total = support_functions.shape[0]
    slot_each = slot_total // N_FN
    rolled = jax.vmap(roll_rows)(support_functions, region_shift).reshape(slot_total, -1)
    starts = jnp.cumsum(owner_counts) - owner_counts
    slot_ids = jnp.arange(slot_total)
    owners = slot_ids // slot_each
    within = slot_ids % slot_each
    global_index = (starts[owners] + within).astype(jnp.int32)
    live_slot = within < owner_counts[owners]
    columns = jnp.where(live_slot[None, :], jnp.take(kernel, jnp.clip(global_index, 0, NF - 1), axis=1), 0.0)
    mixed_rows = jnp.dot(columns, rolled, precision=precise, preferred_element_type=jnp.float32)
    potential_rows = potentials(mixed_rows, external)
    spectral = spectral_bound(kinetic_taps, potential_rows)
    half = NF // 2
    results = []
    for spin in range(2):
        field_rows = mixed_rows[spin * half:(spin + 1) * half].reshape(half, NX, NY, NZ)
        spin_potential = potential_rows[spin].reshape(1, NX, NY, NZ)
        results.append(chebyshev(field_rows, spin_potential, kinetic_taps, magic_taps, spectral))
    return jnp.concatenate(results, axis=0).reshape(NF, NX, NY * NZ)
```

```python
import functools

import jax
import jax.numpy as jnp
from jax import lax
from jax.experimental import pallas as pl
from jax.experimental.pallas import tpu as pltpu
from jax.sharding import PartitionSpec as P

NY = 64
NZ = 32
LANES = 128
SLAB = 256
YS = SLAB // NZ
VMEM = pl.BlockSpec(memory_space=pltpu.VMEM)
SMEM = pl.BlockSpec(memory_space=pltpu.SMEM)
F32 = jnp.float32
BF16 = jnp.bfloat16


def halves(values):
    high = values.astype(BF16)
    low = (values - high.astype(F32)).astype(BF16)
    return high, low


def dot(left, right):
    return jnp.dot(left, right, preferred_element_type=F32)


def params(limit=48 << 20):
    return pltpu.CompilerParams(vmem_limit_bytes=limit)


def roll_kernel(rows_per, shift_ref, slots_ref, own_ref, out_ref, flat_ref):
    slot_each, nx, cells = slots_ref.shape
    q_count = cells // LANES
    unit = min(rows_per, q_count)
    total = nx * q_count
    for s in range(slot_each):
        for q in range(q_count):
            flat_ref[s, pl.ds(q, nx, stride=q_count), :] = slots_ref[s, :, q * LANES:(q + 1) * LANES]
    for s in reversed(range(slot_each)):
        back = shift_ref[s] * q_count
        for u in range(total // unit):
            source = lax.rem(u * unit - back + total, total)
            block = flat_ref[s, pl.ds(pl.multiple_of(source, 8), unit), :]
            dest, within = u * unit // rows_per, u * unit % rows_per
            if s == slot_each - 1:
                out_ref[dest, within:within + unit, :] = block
            else:
                own_ref[dest, s * rows_per + within:s * rows_per + within + unit, :] = block


def matrices_kernel(devices, kin_ref, mag_ref, place_ref, kernel_ref, xf_ref, xb_ref, kin_out, fwd_out, bwd_out, mix_out):
    nx = xb_ref.shape[0]
    kin_half = kin_ref.shape[0]
    taps = mag_ref.shape[0]
    kin_count = 2 * kin_half - 1
    kin_center, mag_center = kin_count // 2, taps // 2
    kin = [-0.5 * kin_ref[abs(t - kin_center)] for t in range(kin_count)]
    mag = [mag_ref[t] for t in range(taps)]
    total = functools.reduce(lambda a, b: a + b, [jnp.abs(m) for m in mag])

    def picked(index, values, first=0):
        summed = jnp.zeros(index.shape, F32)
        for t, value in enumerate(values):
            summed = jnp.where(index == t + first, value, summed)
        return summed

    def iota(shape, dim):
        return lax.broadcasted_iota(jnp.int32, shape, dim)

    spread = max(nx // devices, 1)
    def x_of(row):
        if spread == 1:
            return row
        return lax.rem(row, devices) * spread + row // devices

    out_x, in_x = x_of(iota((nx, nx), 0)), x_of(iota((nx, nx), 1))
    ahead = lax.rem(in_x - out_x + mag_center + nx, nx)
    behind = lax.rem(out_x - in_x + mag_center + nx, nx)
    across = lax.rem(in_x - out_x + kin_center + nx, nx)
    fh, fl = halves(picked(ahead, mag) / total)
    kh, kl = halves(picked(across, kin))
    bh, bl = halves(picked(behind, mag) / total)
    xf_ref[:nx] = jnp.concatenate([fh, fl, fh], axis=1)
    xf_ref[nx:] = jnp.concatenate([kh, kl, kh], axis=1)
    xb_ref[...] = jnp.concatenate([bh, bl, bh], axis=1)

    square = (SLAB, SLAB)
    row, col = iota(square, 0), iota(square, 1)
    in_y, in_z = row // NZ, lax.rem(row, NZ)
    out_y, out_z = col // NZ, lax.rem(col, NZ)
    dy, dz = in_y - out_y, in_z - out_z

    def along_y(delta, values, center, d):
        low = max(YS * d + center - (YS - 1), 0)
        high = min(YS * d + center + YS - 1, len(values) - 1)
        return picked(delta + (YS * d + center), values[low:high + 1], low)

    mag_z = picked(lax.rem(dz + mag_center + NZ, NZ), mag) / total
    mag_zt = picked(lax.rem(mag_center - dz + NZ, NZ), mag) / total
    kin_z = picked(lax.rem(dz + kin_center + NZ, NZ), kin)
    reach = fwd_out.shape[0] // 2 // SLAB // 2
    kin_reach = kin_out.shape[0] // 2 // SLAB // 2
    for n in range(2 * reach + 1):
        d = n - reach
        for out, y_part, z_part in (
            (fwd_out, along_y(dy, mag, mag_center, d), mag_z),
            (bwd_out, along_y(-dy, mag, mag_center, -d), mag_zt),
        ):
            high, low = halves(y_part / total * z_part)
            out[n * SLAB:(n + 1) * SLAB] = high
            base = (2 * reach + 1 + n) * SLAB
            out[base:base + SLAB] = low
    for n in range(2 * kin_reach + 1):
        d = n - kin_reach
        value = jnp.where(dz == 0, along_y(dy, kin, kin_center, d), 0.0)
        if d == 0:
            value = value + jnp.where(dy == 0, kin_z, 0.0)
        high, low = halves(value)
        kin_out[n * SLAB:(n + 1) * SLAB] = high
        base = (2 * kin_reach + 1 + n) * SLAB
        kin_out[base:base + SLAB] = low

    functions = kernel_ref.shape[0]
    local = functions // devices
    full = (functions, functions)
    wanted = lax.rem(iota(full, 0), devices) * local + iota(full, 0) // devices
    row_pick = jnp.where(wanted == iota(full, 1), 1.0, 0.0).astype(BF16)
    col_pick = jnp.where(iota(full, 0) == place_ref[...], 1.0, 0.0).astype(BF16)
    parts = [dot(dot(row_pick, part).astype(BF16), col_pick).astype(BF16) for part in halves(kernel_ref[...])]
    mix_out[...] = jnp.concatenate([parts[0], parts[1], parts[0]], axis=1)


def mix_kernel(devices, arrived_ref, mix_ref, external_ref, out_ref, up_ref, down_ref):
    functions = mix_ref.shape[0]
    local = functions // devices
    rows_per = external_ref.shape[0]
    stride = out_ref.shape[0] // devices
    half = devices // 2
    count = functions // 2
    for c in range(0, rows_per, 2):
        values = jnp.concatenate(
            [arrived_ref[pl.ds(c + k, functions, stride=rows_per), :] for k in range(2)], axis=1
        )
        high, low = halves(values)
        mixed = dot(mix_ref[...], jnp.concatenate([high, high, low], axis=0))
        up = down = 0.0
        for j in range(local):
            part = mixed[j * devices:(j + 1) * devices]
            for k in range(2):
                out_ref[pl.ds(j * rows_per + c + k, devices, stride=stride), :] = part[:, k * LANES:(k + 1) * LANES]
            squared = part * part
            up = up + jnp.sum(squared[:half], axis=0, keepdims=True)
            down = down + jnp.sum(squared[half:], axis=0, keepdims=True)
        for k in range(2):
            up_ref[c + k:c + k + 1, :] = up[:, k * LANES:(k + 1) * LANES]
            down_ref[c + k:c + k + 1, :] = down[:, k * LANES:(k + 1) * LANES]

    def cube_root(x):
        guess = jnp.exp(jnp.log(x) * (1.0 / 3.0))
        return guess - (guess - x / (guess * guess)) * (1.0 / 3.0)

    rho_up, rho_down = up_ref[...] / count, down_ref[...] / count
    shared = external_ref[...] + 0.5 * (rho_up + rho_down)
    spins = [shared - cube_root((6.0 / jnp.pi) * rho + 1e-6) for rho in (rho_up, rho_down)]
    peak = jnp.maximum(jnp.max(jnp.abs(spins[0])), jnp.max(jnp.abs(spins[1])))
    tail = jnp.full((8, LANES), peak, F32)
    for dest in range(devices):
        base = dest * stride + local * rows_per
        out_ref[base:base + rows_per, :] = spins[dest // half]
        out_ref[base + rows_per:base + rows_per + 8, :] = tail


def filter_kernel(devices, rows_per, kin_ref, got_ref, xf_ref, xb_ref, kinm_ref, fwd_ref, bwd_ref, out_ref,
                  v_hi, v_lo, p_hi, p_lo, w_hi, w_lo, acc_ref, pot_ref, stage_ref):
    local, nx, cells = out_ref.shape
    slabs = cells // SLAB
    q_count = cells // LANES
    per_slab = SLAB // LANES
    stride = got_ref.shape[0] // devices
    spread = max(rows_per // q_count, 1)

    def plane(field, q):
        if rows_per >= q_count:
            return jnp.concatenate([
                got_ref[pl.ds(field * rows_per + xo * q_count + q, devices, stride=stride), :]
                for xo in range(spread)
            ], axis=0)
        split = q_count // rows_per
        start = (q // rows_per) * stride + field * rows_per + q % rows_per
        return got_ref[pl.ds(start, nx, stride=split * stride), :]

    def slab_of(field, h):
        return jnp.concatenate([plane(field, h * per_slab + k) for k in range(per_slab)], axis=1)

    for h in range(slabs):
        pot_ref[h] = slab_of(local, h)
        for f in range(local):
            high, low = halves(slab_of(f, h))
            where = slice(f * nx, (f + 1) * nx)
            v_hi[h, where] = high
            v_lo[h, where] = low
            both = dot(xf_ref[...], jnp.concatenate([high, high, low], axis=0))
            p_hi[h, where], p_lo[h, where] = halves(both[:nx])
            acc_ref[h, where] = both[nx:]

    def banded(hi_ref, lo_ref, matrix_ref, h):
        width = matrix_ref.shape[0] // 2
        count = width // SLAB
        places = [lax.rem(h + (n - count // 2) + slabs, slabs) for n in range(count)]
        high = jnp.concatenate([hi_ref[place] for place in places], axis=1)
        low = jnp.concatenate([lo_ref[place] for place in places], axis=1)
        return dot(high, matrix_ref[:width]) + (dot(low, matrix_ref[:width]) + dot(high, matrix_ref[width:]))

    def forward(h, carry):
        acc_ref[h] += banded(v_hi, v_lo, kinm_ref, h)
        smooth = banded(p_hi, p_lo, fwd_ref, h)
        potential = pot_ref[h]
        for f in range(local):
            high, low = halves(smooth[f * nx:(f + 1) * nx] * potential)
            mixed = dot(xb_ref[...], jnp.concatenate([high, high, low], axis=0))
            w_hi[h, f * nx:(f + 1) * nx], w_lo[h, f * nx:(f + 1) * nx] = halves(mixed)
        return carry

    lax.fori_loop(0, slabs, forward, 0)

    sides = jnp.abs(kin_ref[0])
    for t in range(1, kin_ref.shape[0]):
        sides = sides + 2.0 * jnp.abs(kin_ref[t])
    peaks = got_ref[pl.ds((local + 1) * rows_per, devices, stride=stride), :]
    bound = 1.0 + 1.5 * sides + jnp.max(peaks, axis=0, keepdims=True)
    bound = jnp.concatenate([bound] * per_slab, axis=1)

    def backward(h, carry):
        result = (acc_ref[h] + banded(w_hi, w_lo, bwd_ref, h)) / bound
        lanes = pl.multiple_of(h * SLAB, SLAB)
        for f in range(local):
            for xo in range(spread):
                count = nx // spread
                block = result[f * nx + xo * count:f * nx + (xo + 1) * count]
                for k in range(per_slab):
                    stage_ref[f, h * per_slab + k, pl.ds(xo, count, stride=spread), :] = block[:, k * LANES:(k + 1) * LANES]
        for f in range(local):
            for k in range(per_slab):
                out_ref[f, :, pl.ds(pl.multiple_of(lanes + k * LANES, LANES), LANES)] = stage_ref[f, h * per_slab + k]
        return carry

    lax.fori_loop(0, slabs, backward, 0)


def shaped(shape, dtype=F32):
    return jax.ShapeDtypeStruct(shape, dtype)


def body(support_functions, owner_counts, region_shift, kernel, external, kinetic_taps, magic_taps):
    devices = lax.axis_size("fn")
    position = lax.axis_index("fn")
    slot_each, nx, cells = support_functions.shape
    functions = kernel.shape[0]
    local = functions // devices
    rows_per = nx * cells // devices // LANES
    reach = -(-(magic_taps.shape[0] // 2) // YS)
    kin_reach = -(-(kinetic_taps.shape[0] - 1) // YS)

    own, outgoing = pl.pallas_call(
        functools.partial(roll_kernel, rows_per),
        out_shape=(shaped((devices, local * rows_per, LANES)), shaped((devices, rows_per, LANES))),
        in_specs=[SMEM, VMEM],
        out_specs=(VMEM, VMEM),
        scratch_shapes=[pltpu.VMEM((slot_each, nx * cells // LANES, LANES), F32)],
        compiler_params=params(),
        name="roll",
    )(region_shift, support_functions)

    route = [(d, d ^ 1) for d in range(devices)]
    received = lax.ppermute(outgoing, "fn", route)
    lone = owner_counts[position] < local
    balanced = own.at[:, rows_per:].set(jnp.where(lone, received, own[:, rows_per:]))
    arrived = lax.all_to_all(balanced, "fn", split_axis=0, concat_axis=0, tiled=True)

    pairs = jnp.arange(devices // 2, dtype=jnp.int32)[:, None] * (2 * local)
    counts = owner_counts.reshape(-1, 2)
    first = pairs + jnp.concatenate([jnp.zeros_like(counts[:, :1]), counts[:, :1]], axis=1)
    stand_in = pairs + jnp.asarray([[2 * local - 1, local]], jnp.int32)
    second = jnp.where(counts < local, stand_in, first + 1)
    places = jnp.stack([first, second], axis=-1).reshape(1, functions)

    xf, xb, kin_m, fwd_m, bwd_m, mix_m = pl.pallas_call(
        functools.partial(matrices_kernel, devices),
        out_shape=(
            shaped((2 * nx, 3 * nx), BF16),
            shaped((nx, 3 * nx), BF16),
            shaped((2 * (2 * kin_reach + 1) * SLAB, SLAB), BF16),
            shaped((2 * (2 * reach + 1) * SLAB, SLAB), BF16),
            shaped((2 * (2 * reach + 1) * SLAB, SLAB), BF16),
            shaped((functions, 3 * functions), BF16),
        ),
        in_specs=[SMEM, SMEM, VMEM, VMEM],
        out_specs=(VMEM,) * 6,
        compiler_params=params(),
        cost_estimate=pl.CostEstimate(flops=1 << 27, bytes_accessed=4 << 20, transcendentals=0),
        name="matrices",
    )(kinetic_taps, magic_taps, places, kernel)

    stride = (local + 1) * rows_per + 8
    payload = pl.pallas_call(
        functools.partial(mix_kernel, devices),
        out_shape=shaped((devices * stride, LANES)),
        in_specs=[VMEM, VMEM, VMEM],
        out_specs=VMEM,
        scratch_shapes=[pltpu.VMEM((rows_per, LANES), F32)] * 2,
        compiler_params=params(),
        name="mix",
    )(arrived.reshape(-1, LANES), mix_m, external.reshape(rows_per, LANES))

    got = lax.all_to_all(payload.reshape(devices, stride, LANES), "fn", split_axis=0, concat_axis=0, tiled=True)

    slabs = cells // SLAB
    tile = (slabs, local * nx, SLAB)
    return pl.pallas_call(
        functools.partial(filter_kernel, devices, rows_per),
        out_shape=shaped((local, nx, cells)),
        in_specs=[SMEM] + [VMEM] * 6,
        out_specs=VMEM,
        scratch_shapes=[pltpu.VMEM(tile, BF16)] * 6
        + [pltpu.VMEM(tile, F32), pltpu.VMEM((slabs, nx, SLAB), F32),
           pltpu.VMEM((local, cells // LANES, nx, LANES), F32)],
        compiler_params=params(),
        name="filter",
    )(kinetic_taps, got.reshape(-1, LANES), xf, xb, kin_m, fwd_m, bwd_m)


def solution(mesh):
    placed = (P("fn", None, None), P(), P("fn"), P(), P("fn"), P(), P())
    return jax.shard_map(
        body, mesh=mesh, in_specs=placed, out_specs=P("fn", None, None), check_vma=False
    )
```

```python
import functools

import jax
import jax.numpy as jnp
from jax import lax
from jax.experimental import pallas as pl
from jax.experimental.pallas import tpu as pltpu
from jax.sharding import PartitionSpec as P

NY = 64
NZ = 32
LANES = 128
SLAB = 256
YS = SLAB // NZ
VMEM = pl.BlockSpec(memory_space=pltpu.VMEM)
SMEM = pl.BlockSpec(memory_space=pltpu.SMEM)
F32 = jnp.float32
BF16 = jnp.bfloat16


def halves(values):
    high = values.astype(BF16)
    low = (values - high.astype(F32)).astype(BF16)
    return high, low


def dot(left, right):
    return jnp.dot(left, right, preferred_element_type=F32)


def params(**more):
    return pltpu.CompilerParams(vmem_limit_bytes=48 << 20, has_side_effects="collective_id" in more, **more)


def roll_kernel(rows_per, shift_ref, slots_ref, own_ref, out_ref, flat_ref):
    slot_each, nx, cells = slots_ref.shape
    q_count = cells // LANES
    unit = min(rows_per, q_count)
    total = nx * q_count
    for s in range(slot_each):
        for q in range(q_count):
            flat_ref[s, pl.ds(q, nx, stride=q_count), :] = slots_ref[s, :, q * LANES:(q + 1) * LANES]
    for s in reversed(range(slot_each)):
        back = shift_ref[s] * q_count
        for u in range(total // unit):
            source = lax.rem(u * unit - back + total, total)
            block = flat_ref[s, pl.ds(pl.multiple_of(source, 8), unit), :]
            dest, within = u * unit // rows_per, u * unit % rows_per
            if s == slot_each - 1:
                out_ref[dest, within:within + unit, :] = block
            else:
                own_ref[dest, s * rows_per + within:s * rows_per + within + unit, :] = block


def matrices_kernel(devices, kin_ref, mag_ref, place_ref, kernel_ref, xf_ref, xb_ref, kin_out, fwd_out, bwd_out, mix_out):
    nx = xb_ref.shape[0]
    kin_half = kin_ref.shape[0]
    taps = mag_ref.shape[0]
    kin_count = 2 * kin_half - 1
    kin_center, mag_center = kin_count // 2, taps // 2
    kin = [-0.5 * kin_ref[abs(t - kin_center)] for t in range(kin_count)]
    mag = [mag_ref[t] for t in range(taps)]
    total = functools.reduce(lambda a, b: a + b, [jnp.abs(m) for m in mag])

    def picked(index, values, first=0):
        summed = jnp.zeros(index.shape, F32)
        for t, value in enumerate(values):
            summed = jnp.where(index == t + first, value, summed)
        return summed

    def iota(shape, dim):
        return lax.broadcasted_iota(jnp.int32, shape, dim)

    spread = max(nx // devices, 1)
    def x_of(row):
        if spread == 1:
            return row
        return lax.rem(row, devices) * spread + row // devices

    out_x, in_x = x_of(iota((nx, nx), 0)), x_of(iota((nx, nx), 1))
    ahead = lax.rem(in_x - out_x + mag_center + nx, nx)
    behind = lax.rem(out_x - in_x + mag_center + nx, nx)
    across = lax.rem(in_x - out_x + kin_center + nx, nx)
    fh, fl = halves(picked(ahead, mag) / total)
    kh, kl = halves(picked(across, kin))
    bh, bl = halves(picked(behind, mag) / total)
    xf_ref[:nx] = jnp.concatenate([fh, fl, fh], axis=1)
    xf_ref[nx:] = jnp.concatenate([kh, kl, kh], axis=1)
    xb_ref[...] = jnp.concatenate([bh, bl, bh], axis=1)

    square = (SLAB, SLAB)
    row, col = iota(square, 0), iota(square, 1)
    in_y, in_z = row // NZ, lax.rem(row, NZ)
    out_y, out_z = col // NZ, lax.rem(col, NZ)
    dy, dz = in_y - out_y, in_z - out_z

    def along_y(delta, values, center, d):
        low = max(YS * d + center - (YS - 1), 0)
        high = min(YS * d + center + YS - 1, len(values) - 1)
        return picked(delta + (YS * d + center), values[low:high + 1], low)

    mag_z = picked(lax.rem(dz + mag_center + NZ, NZ), mag) / total
    mag_zt = picked(lax.rem(mag_center - dz + NZ, NZ), mag) / total
    kin_z = picked(lax.rem(dz + kin_center + NZ, NZ), kin)
    reach = fwd_out.shape[0] // 2 // SLAB // 2
    kin_reach = kin_out.shape[0] // 2 // SLAB // 2
    for n in range(2 * reach + 1):
        d = n - reach
        for out, y_part, z_part in (
            (fwd_out, along_y(dy, mag, mag_center, d), mag_z),
            (bwd_out, along_y(-dy, mag, mag_center, -d), mag_zt),
        ):
            high, low = halves(y_part / total * z_part)
            out[n * SLAB:(n + 1) * SLAB] = high
            base = (2 * reach + 1 + n) * SLAB
            out[base:base + SLAB] = low
    for n in range(2 * kin_reach + 1):
        d = n - kin_reach
        value = jnp.where(dz == 0, along_y(dy, kin, kin_center, d), 0.0)
        if d == 0:
            value = value + jnp.where(dy == 0, kin_z, 0.0)
        high, low = halves(value)
        kin_out[n * SLAB:(n + 1) * SLAB] = high
        base = (2 * kin_reach + 1 + n) * SLAB
        kin_out[base:base + SLAB] = low

    functions = kernel_ref.shape[0]
    local = functions // devices
    full = (functions, functions)
    wanted = lax.rem(iota(full, 0), devices) * local + iota(full, 0) // devices
    row_pick = jnp.where(wanted == iota(full, 1), 1.0, 0.0).astype(BF16)
    col_pick = jnp.where(iota(full, 0) == place_ref[...], 1.0, 0.0).astype(BF16)
    parts = [dot(dot(row_pick, part).astype(BF16), col_pick).astype(BF16) for part in halves(kernel_ref[...])]
    mix_out[...] = jnp.concatenate([parts[0], parts[1], parts[0]], axis=1)


def partner(me, k):
    bit = 1
    there = me
    while bit <= k:
        if k & bit:
            there = there + bit - 2 * bit * ((me // bit) % 2)
        bit *= 2
    return there


def far_first(devices):
    half = devices // 2
    order = []
    for n in range(half):
        order += [half + n, n]
    return [k for k in order if k]


def greet(me, devices):
    barrier = pltpu.get_barrier_semaphore()
    for k in range(1, devices):
        pl.semaphore_signal(barrier, inc=1, device_id=(partner(me, k),), device_id_type=pl.DeviceIdType.MESH)
    pl.semaphore_wait(barrier, devices - 1)


def remote(source, target, send, recv, device):
    return pltpu.make_async_remote_copy(
        src_ref=source, dst_ref=target, send_sem=send, recv_sem=recv,
        device_id=(device,), device_id_type=pl.DeviceIdType.MESH,
    )


def scatter_kernel(devices, kin_ref, mag_ref, place_ref, kernel_ref, own_ref,
                   xf_ref, xb_ref, kin_out, fwd_out, bwd_out, mix_out, got_ref, send_sem, recv_sem):
    me = lax.axis_index("fn")
    greet(me, devices)
    copies = []
    for k in far_first(devices):
        there = partner(me, k)
        copy = remote(own_ref.at[there], got_ref.at[me], send_sem.at[k], recv_sem.at[k], there)
        copy.start()
        copies.append(copy)
    got_ref[me] = own_ref[me]
    matrices_kernel(devices, kin_ref, mag_ref, place_ref, kernel_ref, xf_ref, xb_ref, kin_out, fwd_out, bwd_out, mix_out)
    for copy in copies:
        copy.wait()


def return_kernel(devices, mixed_ref, pots_ref, got_ref, gpot_ref, send_sem, recv_sem, own_send, own_recv, relay_send, relay_recv):
    me = lax.axis_index("fn")
    half = devices // 2
    side = me // half
    across = partner(me, half)
    greet(me, devices)
    handed = remote(pots_ref.at[1 - side], gpot_ref.at[me], own_send.at[0], own_recv.at[0], across)
    handed.start()
    copies = []
    for k in range(1, half):
        copy = remote(pots_ref.at[side], gpot_ref.at[me], own_send.at[k], own_recv.at[k], partner(me, k))
        copy.start()
        copies.append(copy)
    order = far_first(devices)
    for n, k in enumerate(order):
        there = partner(me, k)
        copy = remote(mixed_ref.at[there], got_ref.at[me], send_sem.at[k], recv_sem.at[k], there)
        copy.start()
        copies.append(copy)
    got_ref[me] = mixed_ref[me]
    gpot_ref[me] = pots_ref[side]
    handed.wait()
    for k in range(1, half):
        copy = remote(gpot_ref.at[across], gpot_ref.at[across], relay_send.at[k], relay_recv.at[k], partner(me, k))
        copy.start()
        copies.append(copy)
    for copy in copies:
        copy.wait()


def mix_kernel(devices, arrived_ref, mix_ref, external_ref, out_ref, pots_ref, up_ref, down_ref):
    functions = mix_ref.shape[0]
    local = functions // devices
    rows_per = external_ref.shape[0]
    stride = out_ref.shape[0] // devices
    half = devices // 2
    count = functions // 2
    for c in range(0, rows_per, 2):
        values = jnp.concatenate(
            [arrived_ref[pl.ds(c + k, functions, stride=rows_per), :] for k in range(2)], axis=1
        )
        high, low = halves(values)
        mixed = dot(mix_ref[...], jnp.concatenate([high, high, low], axis=0))
        up = down = 0.0
        for j in range(local):
            part = mixed[j * devices:(j + 1) * devices]
            for k in range(2):
                out_ref[pl.ds(j * rows_per + c + k, devices, stride=stride), :] = part[:, k * LANES:(k + 1) * LANES]
            squared = part * part
            up = up + jnp.sum(squared[:half], axis=0, keepdims=True)
            down = down + jnp.sum(squared[half:], axis=0, keepdims=True)
        for k in range(2):
            up_ref[c + k:c + k + 1, :] = up[:, k * LANES:(k + 1) * LANES]
            down_ref[c + k:c + k + 1, :] = down[:, k * LANES:(k + 1) * LANES]

    def cube_root(x):
        guess = jnp.exp(jnp.log(x) * (1.0 / 3.0))
        return guess - (guess - x / (guess * guess)) * (1.0 / 3.0)

    rho_up, rho_down = up_ref[...] / count, down_ref[...] / count
    shared = external_ref[...] + 0.5 * (rho_up + rho_down)
    spins = [shared - cube_root((6.0 / jnp.pi) * rho + 1e-6) for rho in (rho_up, rho_down)]
    peak = jnp.maximum(jnp.max(jnp.abs(spins[0])), jnp.max(jnp.abs(spins[1])))
    tail = jnp.full((8, LANES), peak, F32)
    for spin in range(2):
        pots_ref[spin, :rows_per] = spins[spin]
        pots_ref[spin, rows_per:] = tail


def filter_kernel(devices, rows_per, kin_ref, got_ref, gpot_ref, xf_ref, xb_ref, kinm_ref, fwd_ref, bwd_ref, out_ref,
                  v_hi, v_lo, p_hi, p_lo, w_hi, w_lo, acc_ref, pot_ref, stage_ref):
    local, nx, cells = out_ref.shape
    slabs = cells // SLAB
    q_count = cells // LANES
    per_slab = SLAB // LANES
    spread = max(rows_per // q_count, 1)

    def plane(field, q):
        ref, first = (gpot_ref, 0) if field == local else (got_ref, field * rows_per)
        stride = ref.shape[0] // devices
        if rows_per >= q_count:
            return jnp.concatenate([
                ref[pl.ds(first + xo * q_count + q, devices, stride=stride), :] for xo in range(spread)
            ], axis=0)
        split = q_count // rows_per
        start = (q // rows_per) * stride + first + q % rows_per
        return ref[pl.ds(start, nx, stride=split * stride), :]

    def slab_of(field, h):
        return jnp.concatenate([plane(field, h * per_slab + k) for k in range(per_slab)], axis=1)

    for h in range(slabs):
        pot_ref[h] = slab_of(local, h)
        for f in range(local):
            high, low = halves(slab_of(f, h))
            where = slice(f * nx, (f + 1) * nx)
            v_hi[h, where] = high
            v_lo[h, where] = low
            both = dot(xf_ref[...], jnp.concatenate([high, high, low], axis=0))
            p_hi[h, where], p_lo[h, where] = halves(both[:nx])
            acc_ref[h, where] = both[nx:]

    def banded(hi_ref, lo_ref, matrix_ref, h):
        width = matrix_ref.shape[0] // 2
        count = width // SLAB
        places = [lax.rem(h + (n - count // 2) + slabs, slabs) for n in range(count)]
        high = jnp.concatenate([hi_ref[place] for place in places], axis=1)
        low = jnp.concatenate([lo_ref[place] for place in places], axis=1)
        return dot(high, matrix_ref[:width]) + (dot(low, matrix_ref[:width]) + dot(high, matrix_ref[width:]))

    def forward(h, carry):
        acc_ref[h] += banded(v_hi, v_lo, kinm_ref, h)
        smooth = banded(p_hi, p_lo, fwd_ref, h)
        potential = pot_ref[h]
        for f in range(local):
            high, low = halves(smooth[f * nx:(f + 1) * nx] * potential)
            mixed = dot(xb_ref[...], jnp.concatenate([high, high, low], axis=0))
            w_hi[h, f * nx:(f + 1) * nx], w_lo[h, f * nx:(f + 1) * nx] = halves(mixed)
        return carry

    lax.fori_loop(0, slabs, forward, 0)

    sides = jnp.abs(kin_ref[0])
    for t in range(1, kin_ref.shape[0]):
        sides = sides + 2.0 * jnp.abs(kin_ref[t])
    peaks = gpot_ref[pl.ds(rows_per, devices, stride=gpot_ref.shape[0] // devices), :]
    bound = 1.0 + 1.5 * sides + jnp.max(peaks, axis=0, keepdims=True)
    bound = jnp.concatenate([bound] * per_slab, axis=1)

    def backward(h, carry):
        result = (acc_ref[h] + banded(w_hi, w_lo, bwd_ref, h)) / bound
        lanes = pl.multiple_of(h * SLAB, SLAB)
        for f in range(local):
            for xo in range(spread):
                count = nx // spread
                block = result[f * nx + xo * count:f * nx + (xo + 1) * count]
                for k in range(per_slab):
                    stage_ref[f, h * per_slab + k, pl.ds(xo, count, stride=spread), :] = block[:, k * LANES:(k + 1) * LANES]
        for f in range(local):
            for k in range(per_slab):
                out_ref[f, :, pl.ds(pl.multiple_of(lanes + k * LANES, LANES), LANES)] = stage_ref[f, h * per_slab + k]
        return carry

    lax.fori_loop(0, slabs, backward, 0)


def shaped(shape, dtype=F32):
    return jax.ShapeDtypeStruct(shape, dtype)


def body(support_functions, owner_counts, region_shift, kernel, external, kinetic_taps, magic_taps):
    devices = lax.axis_size("fn")
    position = lax.axis_index("fn")
    slot_each, nx, cells = support_functions.shape
    functions = kernel.shape[0]
    local = functions // devices
    rows_per = nx * cells // devices // LANES
    reach = -(-(magic_taps.shape[0] // 2) // YS)
    kin_reach = -(-(kinetic_taps.shape[0] - 1) // YS)

    own, outgoing = pl.pallas_call(
        functools.partial(roll_kernel, rows_per),
        out_shape=(shaped((devices, local * rows_per, LANES)), shaped((devices, rows_per, LANES))),
        in_specs=[SMEM, VMEM],
        out_specs=(VMEM, VMEM),
        scratch_shapes=[pltpu.VMEM((slot_each, nx * cells // LANES, LANES), F32)],
        compiler_params=params(),
        name="roll",
    )(region_shift, support_functions)

    route = [(d, d ^ 1) for d in range(devices)]
    received = lax.ppermute(outgoing, "fn", route)
    lone = owner_counts[position] < local
    balanced = own.at[:, rows_per:].set(jnp.where(lone, received, own[:, rows_per:]))

    pairs = jnp.arange(devices // 2, dtype=jnp.int32)[:, None] * (2 * local)
    counts = owner_counts.reshape(-1, 2)
    first = pairs + jnp.concatenate([jnp.zeros_like(counts[:, :1]), counts[:, :1]], axis=1)
    stand_in = pairs + jnp.asarray([[2 * local - 1, local]], jnp.int32)
    second = jnp.where(counts < local, stand_in, first + 1)
    places = jnp.stack([first, second], axis=-1).reshape(1, functions)

    each = pltpu.SemaphoreType.DMA((devices,))
    xf, xb, kin_m, fwd_m, bwd_m, mix_m, arrived = pl.pallas_call(
        functools.partial(scatter_kernel, devices),
        out_shape=(
            shaped((2 * nx, 3 * nx), BF16),
            shaped((nx, 3 * nx), BF16),
            shaped((2 * (2 * kin_reach + 1) * SLAB, SLAB), BF16),
            shaped((2 * (2 * reach + 1) * SLAB, SLAB), BF16),
            shaped((2 * (2 * reach + 1) * SLAB, SLAB), BF16),
            shaped((functions, 3 * functions), BF16),
            shaped((devices, local * rows_per, LANES)),
        ),
        in_specs=[SMEM, SMEM, VMEM, VMEM, VMEM],
        out_specs=(VMEM,) * 7,
        scratch_shapes=[each, each],
        compiler_params=params(collective_id=0),
        name="scatter",
    )(kinetic_taps, magic_taps, places, kernel, balanced)

    mixed, pots = pl.pallas_call(
        functools.partial(mix_kernel, devices),
        out_shape=(shaped((devices * local * rows_per, LANES)), shaped((2, rows_per + 8, LANES))),
        in_specs=[VMEM, VMEM, VMEM],
        out_specs=(VMEM, VMEM),
        scratch_shapes=[pltpu.VMEM((rows_per, LANES), F32)] * 2,
        compiler_params=params(),
        name="mix",
    )(arrived.reshape(-1, LANES), mix_m, external.reshape(rows_per, LANES))

    got, gpot = pl.pallas_call(
        functools.partial(return_kernel, devices),
        out_shape=(shaped((devices, local * rows_per, LANES)), shaped((devices, rows_per + 8, LANES))),
        in_specs=[VMEM, VMEM],
        out_specs=(VMEM, VMEM),
        scratch_shapes=[each] * 6,
        compiler_params=params(collective_id=1),
        name="give_back",
    )(mixed.reshape(devices, local * rows_per, LANES), pots)

    slabs = cells // SLAB
    tile = (slabs, local * nx, SLAB)
    return pl.pallas_call(
        functools.partial(filter_kernel, devices, rows_per),
        out_shape=shaped((local, nx, cells)),
        in_specs=[SMEM] + [VMEM] * 7,
        out_specs=VMEM,
        scratch_shapes=[pltpu.VMEM(tile, BF16)] * 6
        + [pltpu.VMEM(tile, F32), pltpu.VMEM((slabs, nx, SLAB), F32),
           pltpu.VMEM((local, cells // LANES, nx, LANES), F32)],
        compiler_params=params(),
        name="filter",
    )(kinetic_taps, got.reshape(-1, LANES), gpot.reshape(-1, LANES), xf, xb, kin_m, fwd_m, bwd_m)


def solution(mesh):
    placed = (P("fn", None, None), P(), P("fn"), P(), P("fn"), P(), P())
    return jax.shard_map(
        body, mesh=mesh, in_specs=placed, out_specs=P("fn", None, None), check_vma=False
    )
```

```python
import functools

import jax
import jax.numpy as jnp
from jax import lax
from jax.experimental import pallas as pl
from jax.experimental.pallas import tpu as pltpu
from jax.sharding import PartitionSpec as P

NY = 64
NZ = 32
LANES = 128
SLAB = 256
YS = SLAB // NZ
GROUP = 4
VMEM = pl.BlockSpec(memory_space=pltpu.VMEM)
SMEM = pl.BlockSpec(memory_space=pltpu.SMEM)
F32 = jnp.float32
BF16 = jnp.bfloat16


def halves(values):
    high = values.astype(BF16)
    low = (values - high.astype(F32)).astype(BF16)
    return high, low


def dot(left, right):
    return jnp.dot(left, right, preferred_element_type=F32)


def params(**more):
    return pltpu.CompilerParams(vmem_limit_bytes=48 << 20, has_side_effects="collective_id" in more, **more)


def roll_kernel(rows_per, shift_ref, slots_ref, own_ref, out_ref, flat_ref):
    slot_each, nx, cells = slots_ref.shape
    q_count = cells // LANES
    unit = min(rows_per, q_count)
    total = nx * q_count
    for s in range(slot_each):
        for q in range(q_count):
            flat_ref[s, pl.ds(q, nx, stride=q_count), :] = slots_ref[s, :, q * LANES:(q + 1) * LANES]
    for s in reversed(range(slot_each)):
        back = shift_ref[s] * q_count
        for u in range(total // unit):
            source = lax.rem(u * unit - back + total, total)
            block = flat_ref[s, pl.ds(pl.multiple_of(source, 8), unit), :]
            dest, within = u * unit // rows_per, u * unit % rows_per
            if s == slot_each - 1:
                out_ref[dest, within:within + unit, :] = block
            else:
                own_ref[dest, s * rows_per + within:s * rows_per + within + unit, :] = block


def matrices_kernel(devices, kin_ref, mag_ref, place_ref, kernel_ref, xf_ref, xb_ref, kin_out, fwd_out, bwd_out, mix_out):
    nx = xb_ref.shape[0]
    kin_half = kin_ref.shape[0]
    taps = mag_ref.shape[0]
    kin_count = 2 * kin_half - 1
    kin_center, mag_center = kin_count // 2, taps // 2
    kin = [-0.5 * kin_ref[abs(t - kin_center)] for t in range(kin_count)]
    mag = [mag_ref[t] for t in range(taps)]
    total = functools.reduce(lambda a, b: a + b, [jnp.abs(m) for m in mag])

    def picked(index, values, first=0):
        summed = jnp.zeros(index.shape, F32)
        for t, value in enumerate(values):
            summed = jnp.where(index == t + first, value, summed)
        return summed

    def iota(shape, dim):
        return lax.broadcasted_iota(jnp.int32, shape, dim)

    spread = max(nx // devices, 1)
    def x_of(row):
        if spread == 1:
            return row
        return lax.rem(row, devices) * spread + row // devices

    out_x, in_x = x_of(iota((nx, nx), 0)), x_of(iota((nx, nx), 1))
    ahead = lax.rem(in_x - out_x + mag_center + nx, nx)
    behind = lax.rem(out_x - in_x + mag_center + nx, nx)
    across = lax.rem(in_x - out_x + kin_center + nx, nx)
    fh, fl = halves(picked(ahead, mag) / total)
    kh, kl = halves(picked(across, kin))
    bh, bl = halves(picked(behind, mag) / total)
    xf_ref[:nx] = jnp.concatenate([fh, fl, fh], axis=1)
    xf_ref[nx:] = jnp.concatenate([kh, kl, kh], axis=1)
    xb_ref[...] = jnp.concatenate([bh, bl, bh], axis=1)

    square = (SLAB, SLAB)
    row, col = iota(square, 0), iota(square, 1)
    in_y, in_z = row // NZ, lax.rem(row, NZ)
    out_y, out_z = col // NZ, lax.rem(col, NZ)
    dy, dz = in_y - out_y, in_z - out_z

    def along_y(delta, values, center, d):
        low = max(YS * d + center - (YS - 1), 0)
        high = min(YS * d + center + YS - 1, len(values) - 1)
        return picked(delta + (YS * d + center), values[low:high + 1], low)

    mag_z = picked(lax.rem(dz + mag_center + NZ, NZ), mag) / total
    mag_zt = picked(lax.rem(mag_center - dz + NZ, NZ), mag) / total
    kin_z = picked(lax.rem(dz + kin_center + NZ, NZ), kin)
    reach = fwd_out.shape[0] // 2 // SLAB // 2
    kin_reach = kin_out.shape[0] // 2 // SLAB // 2
    for n in range(2 * reach + 1):
        d = n - reach
        for out, y_part, z_part in (
            (fwd_out, along_y(dy, mag, mag_center, d), mag_z),
            (bwd_out, along_y(-dy, mag, mag_center, -d), mag_zt),
        ):
            high, low = halves(y_part / total * z_part)
            out[n * SLAB:(n + 1) * SLAB] = high
            base = (2 * reach + 1 + n) * SLAB
            out[base:base + SLAB] = low
    for n in range(2 * kin_reach + 1):
        d = n - kin_reach
        value = jnp.where(dz == 0, along_y(dy, kin, kin_center, d), 0.0)
        if d == 0:
            value = value + jnp.where(dy == 0, kin_z, 0.0)
        high, low = halves(value)
        kin_out[n * SLAB:(n + 1) * SLAB] = high
        base = (2 * kin_reach + 1 + n) * SLAB
        kin_out[base:base + SLAB] = low

    functions = kernel_ref.shape[0]
    local = functions // devices
    full = (functions, functions)
    wanted = lax.rem(iota(full, 0), devices) * local + iota(full, 0) // devices
    row_pick = jnp.where(wanted == iota(full, 1), 1.0, 0.0).astype(BF16)
    col_pick = jnp.where(iota(full, 0) == place_ref[...], 1.0, 0.0).astype(BF16)
    parts = [dot(dot(row_pick, part).astype(BF16), col_pick).astype(BF16) for part in halves(kernel_ref[...])]
    mix_out[...] = jnp.concatenate([parts[0], parts[1], parts[0]], axis=1)


def partner(me, k):
    bit = 1
    there = me
    while bit <= k:
        if k & bit:
            there = there + bit - 2 * bit * ((me // bit) % 2)
        bit *= 2
    return there


def far_first(devices):
    half = devices // 2
    order = []
    for n in range(half):
        order += [half + n, n]
    return [k for k in order if k]


def greet(me, devices):
    barrier = pltpu.get_barrier_semaphore()
    for k in range(1, devices):
        pl.semaphore_signal(barrier, inc=1, device_id=(partner(me, k),), device_id_type=pl.DeviceIdType.MESH)
    pl.semaphore_wait(barrier, devices - 1)


def remote(source, target, send, recv, device):
    return pltpu.make_async_remote_copy(
        src_ref=source, dst_ref=target, send_sem=send, recv_sem=recv,
        device_id=(device,), device_id_type=pl.DeviceIdType.MESH,
    )


def scatter_kernel(devices, kin_ref, mag_ref, place_ref, kernel_ref, own_ref,
                   xf_ref, xb_ref, kin_out, fwd_out, bwd_out, mix_out, got_ref, send_sem, recv_sem):
    me = lax.axis_index("fn")
    greet(me, devices)
    copies = []
    for k in far_first(devices):
        there = partner(me, k)
        copy = remote(own_ref.at[there], got_ref.at[me], send_sem.at[k], recv_sem.at[k], there)
        copy.start()
        copies.append(copy)
    got_ref[me] = own_ref[me]
    matrices_kernel(devices, kin_ref, mag_ref, place_ref, kernel_ref, xf_ref, xb_ref, kin_out, fwd_out, bwd_out, mix_out)
    for copy in copies:
        copy.wait()


def return_kernel(devices, mixed_ref, pots_ref, got_ref, gpot_ref, send_sem, recv_sem, own_send, own_recv,
                  relay_send, relay_recv, core_send, core_recv):
    me = lax.axis_index("fn")
    half = devices // 2
    side = me // half
    across = partner(me, half)
    other_core = partner(me, 1)
    greet(me, devices)

    def to_core(source, owner, k):
        copy = remote(source, gpot_ref.at[owner], core_send.at[k], core_recv.at[k], other_core)
        copy.start()
        return copy

    handed = remote(pots_ref.at[1 - side], gpot_ref.at[me], own_send.at[0], own_recv.at[0], across)
    handed.start()
    direct, relays, blocks, core = {}, {}, [], []
    for k in range(2, half, 2):
        direct[k] = remote(pots_ref.at[side], gpot_ref.at[me], own_send.at[k], own_recv.at[k], partner(me, k))
        direct[k].start()
    core.append(to_core(pots_ref.at[side], me, 0))

    def give(ks):
        for k in ks:
            there = partner(me, k)
            copy = remote(mixed_ref.at[there], got_ref.at[me], send_sem.at[k], recv_sem.at[k], there)
            copy.start()
            blocks.append(copy)

    order = far_first(devices)
    ahead = len(order) // 3
    give(order[:ahead])
    handed.wait()
    for k in range(2, half, 2):
        relays[k] = remote(gpot_ref.at[across], gpot_ref.at[across], relay_send.at[k], relay_recv.at[k], partner(me, k))
        relays[k].start()
    core.append(to_core(gpot_ref.at[across], across, half))
    give(order[ahead:])
    got_ref[me] = mixed_ref[me]
    gpot_ref[me] = pots_ref[side]
    for k, copy in direct.items():
        copy.wait_recv()
        owner = partner(me, k)
        core.append(to_core(gpot_ref.at[owner], owner, k))
    for k, copy in relays.items():
        copy.wait_recv()
        owner = partner(me, k + half)
        core.append(to_core(gpot_ref.at[owner], owner, k + half))
    for copy in [*direct.values(), *relays.values()]:
        copy.wait_send()
    for copy in blocks + core:
        copy.wait()


def mix_kernel(devices, arrived_ref, mix_ref, external_ref, out_ref, pots_ref, up_ref, down_ref):
    functions = mix_ref.shape[0]
    local = functions // devices
    rows_per = external_ref.shape[0]
    stride = out_ref.shape[0] // devices
    half = devices // 2
    count = functions // 2
    for c in range(0, rows_per, 2):
        values = jnp.concatenate(
            [arrived_ref[pl.ds(c + k, functions, stride=rows_per), :] for k in range(2)], axis=1
        )
        high, low = halves(values)
        mixed = dot(mix_ref[...], jnp.concatenate([high, high, low], axis=0))
        up = down = 0.0
        for j in range(local):
            part = mixed[j * devices:(j + 1) * devices]
            for k in range(2):
                out_ref[pl.ds(j * rows_per + c + k, devices, stride=stride), :] = part[:, k * LANES:(k + 1) * LANES]
            squared = part * part
            up = up + jnp.sum(squared[:half], axis=0, keepdims=True)
            down = down + jnp.sum(squared[half:], axis=0, keepdims=True)
        for k in range(2):
            up_ref[c + k:c + k + 1, :] = up[:, k * LANES:(k + 1) * LANES]
            down_ref[c + k:c + k + 1, :] = down[:, k * LANES:(k + 1) * LANES]

    def cube_root(x):
        guess = jnp.exp(jnp.log(x) * (1.0 / 3.0))
        return guess - (guess - x / (guess * guess)) * (1.0 / 3.0)

    rho_up, rho_down = up_ref[...] / count, down_ref[...] / count
    shared = external_ref[...] + 0.5 * (rho_up + rho_down)
    spins = [shared - cube_root((6.0 / jnp.pi) * rho + 1e-6) for rho in (rho_up, rho_down)]
    peak = jnp.maximum(jnp.max(jnp.abs(spins[0])), jnp.max(jnp.abs(spins[1])))
    tail = jnp.full((8, LANES), peak, F32)
    for spin in range(2):
        pots_ref[spin, :rows_per] = spins[spin]
        pots_ref[spin, rows_per:] = tail


def filter_kernel(devices, rows_per, kin_ref, got_ref, gpot_ref, xf_ref, xb_ref, kinm_ref, fwd_ref, bwd_ref, out_ref,
                  v_hi, v_lo, p_hi, p_lo, w_hi, w_lo, acc_ref, pot_ref, stage_ref):
    local, nx, cells = out_ref.shape
    slabs = cells // SLAB
    q_count = cells // LANES
    per_slab = SLAB // LANES
    spread = max(rows_per // q_count, 1)

    def plane(field, q):
        ref, first = (gpot_ref, 0) if field == local else (got_ref, field * rows_per)
        stride = ref.shape[0] // devices
        if rows_per >= q_count:
            return jnp.concatenate([
                ref[pl.ds(first + xo * q_count + q, devices, stride=stride), :] for xo in range(spread)
            ], axis=0)
        split = q_count // rows_per
        start = (q // rows_per) * stride + first + q % rows_per
        return ref[pl.ds(start, nx, stride=split * stride), :]

    def slab_of(field, h):
        return jnp.concatenate([plane(field, h * per_slab + k) for k in range(per_slab)], axis=1)

    for h in range(slabs):
        pot_ref[h] = slab_of(local, h)
        for f in range(local):
            high, low = halves(slab_of(f, h))
            where = slice(f * nx, (f + 1) * nx)
            v_hi[h, where] = high
            v_lo[h, where] = low
            both = dot(xf_ref[...], jnp.concatenate([high, high, low], axis=0))
            p_hi[h, where], p_lo[h, where] = halves(both[:nx])
            acc_ref[h, where] = both[nx:]

    def banded(hi_ref, lo_ref, matrix_ref, h):
        width = matrix_ref.shape[0] // 2
        count = width // SLAB

        def wide(ref):
            return jnp.concatenate([
                jnp.concatenate(
                    [ref[lax.rem(h + g + (n - count // 2) + slabs, slabs)] for n in range(count)], axis=1
                ) for g in range(GROUP)
            ], axis=0)

        high, low = wide(hi_ref), wide(lo_ref)
        return dot(high, matrix_ref[:width]) + (dot(low, matrix_ref[:width]) + dot(high, matrix_ref[width:]))

    def forward(step, carry):
        h = step * GROUP
        kinetic = banded(v_hi, v_lo, kinm_ref, h)
        smooth = banded(p_hi, p_lo, fwd_ref, h)
        for g in range(GROUP):
            base = g * local * nx
            acc_ref[h + g] += kinetic[base:base + local * nx]
            potential = pot_ref[h + g]
            for f in range(local):
                high, low = halves(smooth[base + f * nx:base + (f + 1) * nx] * potential)
                mixed = dot(xb_ref[...], jnp.concatenate([high, high, low], axis=0))
                w_hi[h + g, f * nx:(f + 1) * nx], w_lo[h + g, f * nx:(f + 1) * nx] = halves(mixed)
        return carry

    lax.fori_loop(0, slabs // GROUP, forward, 0)

    sides = jnp.abs(kin_ref[0])
    for t in range(1, kin_ref.shape[0]):
        sides = sides + 2.0 * jnp.abs(kin_ref[t])
    peaks = gpot_ref[pl.ds(rows_per, devices, stride=gpot_ref.shape[0] // devices), :]
    bound = 1.0 + 1.5 * sides + jnp.max(peaks, axis=0, keepdims=True)
    bound = jnp.concatenate([bound] * per_slab, axis=1)

    def backward(step, carry):
        first = step * GROUP
        back = banded(w_hi, w_lo, bwd_ref, first)
        count = nx // spread
        for g in range(GROUP):
            h = first + g
            result = (acc_ref[h] + back[g * local * nx:(g + 1) * local * nx]) / bound
            for f in range(local):
                for k in range(per_slab):
                    q = h * per_slab + k
                    if spread > 1:
                        for xo in range(spread):
                            block = result[f * nx + xo * count:f * nx + (xo + 1) * count, k * LANES:(k + 1) * LANES]
                            stage_ref[f, q, pl.ds(xo, count, stride=spread), :] = block
                        ordered = stage_ref[f, q]
                    else:
                        ordered = result[f * nx:(f + 1) * nx, k * LANES:(k + 1) * LANES]
                    out_ref[f, :, pl.ds(pl.multiple_of(q * LANES, LANES), LANES)] = ordered
        return carry

    lax.fori_loop(0, slabs // GROUP, backward, 0)


def shaped(shape, dtype=F32):
    return jax.ShapeDtypeStruct(shape, dtype)


def body(support_functions, owner_counts, region_shift, kernel, external, kinetic_taps, magic_taps):
    devices = lax.axis_size("fn")
    position = lax.axis_index("fn")
    slot_each, nx, cells = support_functions.shape
    functions = kernel.shape[0]
    local = functions // devices
    rows_per = nx * cells // devices // LANES
    reach = -(-(magic_taps.shape[0] // 2) // YS)
    kin_reach = -(-(kinetic_taps.shape[0] - 1) // YS)

    own, outgoing = pl.pallas_call(
        functools.partial(roll_kernel, rows_per),
        out_shape=(shaped((devices, local * rows_per, LANES)), shaped((devices, rows_per, LANES))),
        in_specs=[SMEM, VMEM],
        out_specs=(VMEM, VMEM),
        scratch_shapes=[pltpu.VMEM((slot_each, nx * cells // LANES, LANES), F32)],
        compiler_params=params(),
        name="roll",
    )(region_shift, support_functions)

    route = [(d, d ^ 1) for d in range(devices)]
    received = lax.ppermute(outgoing, "fn", route)
    lone = owner_counts[position] < local
    balanced = own.at[:, rows_per:].set(jnp.where(lone, received, own[:, rows_per:]))

    pairs = jnp.arange(devices // 2, dtype=jnp.int32)[:, None] * (2 * local)
    counts = owner_counts.reshape(-1, 2)
    first = pairs + jnp.concatenate([jnp.zeros_like(counts[:, :1]), counts[:, :1]], axis=1)
    stand_in = pairs + jnp.asarray([[2 * local - 1, local]], jnp.int32)
    second = jnp.where(counts < local, stand_in, first + 1)
    places = jnp.stack([first, second], axis=-1).reshape(1, functions)

    each = pltpu.SemaphoreType.DMA((devices,))
    xf, xb, kin_m, fwd_m, bwd_m, mix_m, arrived = pl.pallas_call(
        functools.partial(scatter_kernel, devices),
        out_shape=(
            shaped((2 * nx, 3 * nx), BF16),
            shaped((nx, 3 * nx), BF16),
            shaped((2 * (2 * kin_reach + 1) * SLAB, SLAB), BF16),
            shaped((2 * (2 * reach + 1) * SLAB, SLAB), BF16),
            shaped((2 * (2 * reach + 1) * SLAB, SLAB), BF16),
            shaped((functions, 3 * functions), BF16),
            shaped((devices, local * rows_per, LANES)),
        ),
        in_specs=[SMEM, SMEM, VMEM, VMEM, VMEM],
        out_specs=(VMEM,) * 7,
        scratch_shapes=[each, each],
        compiler_params=params(collective_id=0),
        name="scatter",
    )(kinetic_taps, magic_taps, places, kernel, balanced)

    mixed, pots = pl.pallas_call(
        functools.partial(mix_kernel, devices),
        out_shape=(shaped((devices * local * rows_per, LANES)), shaped((2, rows_per + 8, LANES))),
        in_specs=[VMEM, VMEM, VMEM],
        out_specs=(VMEM, VMEM),
        scratch_shapes=[pltpu.VMEM((rows_per, LANES), F32)] * 2,
        compiler_params=params(),
        name="mix",
    )(arrived.reshape(-1, LANES), mix_m, external.reshape(rows_per, LANES))

    got, gpot = pl.pallas_call(
        functools.partial(return_kernel, devices),
        out_shape=(shaped((devices, local * rows_per, LANES)), shaped((devices, rows_per + 8, LANES))),
        in_specs=[VMEM, VMEM],
        out_specs=(VMEM, VMEM),
        scratch_shapes=[each] * 8,
        compiler_params=params(collective_id=1),
        name="give_back",
    )(mixed.reshape(devices, local * rows_per, LANES), pots)

    slabs = cells // SLAB
    tile = (slabs, local * nx, SLAB)
    return pl.pallas_call(
        functools.partial(filter_kernel, devices, rows_per),
        out_shape=shaped((local, nx, cells)),
        in_specs=[SMEM] + [VMEM] * 7,
        out_specs=VMEM,
        scratch_shapes=[pltpu.VMEM(tile, BF16)] * 6
        + [pltpu.VMEM(tile, F32), pltpu.VMEM((slabs, nx, SLAB), F32),
           pltpu.VMEM((local, cells // LANES, nx, LANES), F32)],
        compiler_params=params(),
        name="filter",
    )(kinetic_taps, got.reshape(-1, LANES), gpot.reshape(-1, LANES), xf, xb, kin_m, fwd_m, bwd_m)


def solution(mesh):
    placed = (P("fn", None, None), P(), P("fn"), P(), P("fn"), P(), P())
    return jax.shard_map(
        body, mesh=mesh, in_specs=placed, out_specs=P("fn", None, None), check_vma=False
    )
```
